32 devices in a mesh: dp: 4 (over y, x), fsdp: 8 (over z, core).
Axes of the slice: x: 2, y: 2, z: 4, core: 2. Of those that a mesh axis runs over, the one named last changes fastest.
Arguments:
- dec_in: bfloat16 [64, 384, 1472], P(('dp', 'fsdp')), may hold values from -6 to 6
- enc_out: bfloat16 [64, 256, 1472], P(('dp', 'fsdp')), may hold values from -6 to 6
- d_out: bfloat16 [64, 384, 1472], P(('dp', 'fsdp')), may hold values from -6 to 6
- cont_len: int32 [64, 2], P(('dp', 'fsdp')), may hold values from 1 to 96, 128 in all within a row
- buckets: int32 [352], replicated, may hold values from 0 to 31, as said below
- self_qkv: bfloat16 [1472, 1152], P('fsdp', 'dp'), may hold values from -0.078125 to 0.078125
- self_out: bfloat16 [384, 1472], P('fsdp', 'dp'), may hold values from -1.25 to 1.25
- cross_q: bfloat16 [1472, 384], P('fsdp', 'dp'), may hold values from -0.078125 to 0.078125
- cross_kv: bfloat16 [1472, 768], P('fsdp', 'dp'), may hold values from -0.078125 to 0.078125
- cross_out: bfloat16 [384, 1472], P('fsdp', 'dp'), may hold values from -1.75 to 1.75
- ff_in: bfloat16 [1472, 7168], P('fsdp', 'dp'), may hold values from -0.15625 to 0.15625
- ff_out: bfloat16 [3584, 1472], P('fsdp', 'dp'), may hold values from -0.09375 to 0.09375
- gain_self: bfloat16 [1472], P('fsdp'), may hold values from 0.25 to 1.75
- gain_cross: bfloat16 [1472], P('fsdp'), may hold values from 0.25 to 1.75
- gain_ff: bfloat16 [1472], P('fsdp'), may hold values from 0.25 to 1.75
- rel_bias: bfloat16 [32, 6], P('fsdp'), may hold values from -4 to 4
Outputs:
- out: bfloat16 [64, 384, 1472], P(('dp', 'fsdp'))
- d_dec: bfloat16 [64, 384, 1472], P(('dp', 'fsdp'))
- d_enc: bfloat16 [64, 256, 1472], P(('dp', 'fsdp'))
- d_self_qkv: float32 [1472, 1152], P('fsdp', 'dp')
- d_self_out: float32 [384, 1472], P('fsdp', 'dp')
- d_cross_q: float32 [1472, 384], P('fsdp', 'dp')
- d_cross_kv: float32 [1472, 768], P('fsdp', 'dp')
- d_cross_out: float32 [384, 1472], P('fsdp', 'dp')
- d_ff_in: float32 [1472, 7168], P('fsdp', 'dp')
- d_ff_out: float32 [3584, 1472], P('fsdp', 'dp')
- d_gain_self: float32 [1472], P('fsdp')
- d_gain_cross: float32 [1472], P('fsdp')
- d_gain_ff: float32 [1472], P('fsdp')
- d_rel_bias: float32 [32, 6], P('fsdp')
The draws below stay inside these ranges and needn't reach their ends.
Inputs may be any that keep to these rules, and one draw needn't show every extreme that they name: `cont_len`: the 2 lengths of a group sum to 128, and neither exceeds 96. `buckets`: Non-decreasing over the distance; the first entry is 0 and the last is 31.
All inputs are finite; a program needn't handle non-finite values.
Results may differ from the reference program's by a relative error of at most 0.03.
Values may be sent and summed in bfloat16 or wider, within the bound.
A program may use at most 256 MiB of HBM per device.

```python
import math
from functools import partial
import jax
import jax.numpy as jnp
import numpy as np
from jax import lax

D = 1472
HEADS = 6
DK = 64
FF = 3584
BUCKETS = 32
PROMPT = 256
CONT = 2
CONT_TOK = 128
CMOST = 96
ENC = 256
INNER = 384
GTOK = 384
DIST = 352
GROUPS = 64


def draw_buckets(key, part):
    middle = jnp.sort(jax.random.randint(key, (DIST - 2,), 0, BUCKETS)).astype(jnp.int32)
    return jnp.concatenate([jnp.zeros((1,), jnp.int32), middle, jnp.full((1,), BUCKETS - 1, jnp.int32)])


def levels(key, shape, pieces, smallest, largest):
    loudness = 1.0
    for dim, blocks in pieces:
        steps = jax.random.uniform(jax.random.fold_in(jax.random.fold_in(key, 6), dim), (blocks,), jnp.float32, smallest / len(pieces), largest / len(pieces))
        loudness = loudness * jnp.repeat(jnp.exp(steps), shape[dim] // blocks).reshape((-1,) + (1,) * (len(shape) - 1 - dim))
    return loudness


def profile(number_of, total, reach, skew):
    loads = [(1 << 20) // math.isqrt(grade ** skew) + 1 for grade in range(2, number_of + 1)]
    rest, holding = total - reach - (number_of - 1), [1] * (number_of - 1)
    while rest > 0:
        movable = [i for i in range(number_of - 1) if holding[i] < reach]
        mass, remaining = sum([loads[i] for i in movable]), rest
        for i in movable:
            more = min(reach - holding[i], max(1, remaining * loads[i] // mass), rest)
            holding[i] = holding[i] + more
            rest = rest - more
    return np.array([reach] + holding)


def ragged(stream_key, amount, total, most, lean):
    if amount == 2:
        one = jax.random.randint(stream_key, (), max(1, total - most), min(most, total - 1) + 1)
        return jnp.stack([one, total - one])
    sizes = jnp.asarray(profile(amount, total, most, lean), jnp.int32)
    twos = (amount - 1) // 2
    donor, sink = sizes[1:1 + 2 * twos:2], sizes[2:2 + 2 * twos:2]
    room = jnp.minimum(donor - 1, most - sink)
    shifted = jax.random.randint(jax.random.fold_in(stream_key, 1), (twos,), 0, 1 << 20) % (room + 1)
    sizes = sizes.at[1:1 + 2 * twos:2].set(donor - shifted).at[2:2 + 2 * twos:2].set(sink + shifted)
    return sizes[jax.random.permutation(jax.random.fold_in(stream_key, 2), amount)]


def bell_draw(rng, extent, spread, reach, cuts=(), kind=jnp.bfloat16):
    level = levels(rng, extent, cuts, -0.22, 0.18) if cuts else 1.0
    result = jax.random.normal(rng, extent, jnp.float32) * spread * level
    return jnp.minimum(jnp.maximum(result, -reach), reach).astype(kind)


def setup_inputs(seed: int = 0) -> dict:
    arg_keys = jax.random.split(jax.random.key(seed), 17)
    return {
        "dec_in": bell_draw(arg_keys[0], (GROUPS, GTOK, D), 1.0, 6.0, ((0, 32),)),
        "enc_out": bell_draw(arg_keys[1], (GROUPS, ENC, D), 1.0, 6.0, ((0, 32),)),
        "d_out": bell_draw(arg_keys[2], (GROUPS, GTOK, D), 1.0, 6.0, ((0, 32),)),
        "cont_len": jax.vmap(lambda own: ragged(own, CONT, CONT_TOK, CMOST, 2))(jax.random.split(arg_keys[3], GROUPS)).reshape((GROUPS, CONT)).astype(jnp.int32),
        "buckets": draw_buckets(jax.random.fold_in(arg_keys[16], 71), 0),
        "self_qkv": bell_draw(arg_keys[5], (D, 3 * INNER), (4 * D) ** -0.5, 0.078125, ((0, 8), (1, 4))),
        "self_out": bell_draw(arg_keys[6], (INNER, D), (INNER // 16) ** -0.5, 1.25, ((0, 8), (1, 4))),
        "cross_q": bell_draw(arg_keys[7], (D, INNER), (4 * D) ** -0.5, 0.078125, ((0, 8), (1, 4))),
        "cross_kv": bell_draw(arg_keys[8], (D, 2 * INNER), (4 * D) ** -0.5, 0.078125, ((0, 8), (1, 4))),
        "cross_out": bell_draw(arg_keys[9], (INNER, D), (INNER // 32) ** -0.5, 1.75, ((0, 8), (1, 4))),
        "ff_in": bell_draw(arg_keys[10], (D, 2 * FF), D ** -0.5, 0.15625, ((0, 8), (1, 4))),
        "ff_out": bell_draw(arg_keys[11], (FF, D), FF ** -0.5, 0.09375, ((0, 8), (1, 4))),
        "gain_self": jnp.clip(1.0 + 0.15 * jax.random.normal(arg_keys[12], (D,), jnp.float32), 0.25, 1.75).astype(jnp.bfloat16),
        "gain_cross": jnp.clip(1.0 + 0.15 * jax.random.normal(arg_keys[13], (D,), jnp.float32), 0.25, 1.75).astype(jnp.bfloat16),
        "gain_ff": jnp.clip(1.0 + 0.15 * jax.random.normal(arg_keys[14], (D,), jnp.float32), 0.25, 1.75).astype(jnp.bfloat16),
        "rel_bias": bell_draw(arg_keys[15], (BUCKETS, HEADS), 1.0, 4.0, ((0, 8),)),
    }


EPSILON = 1e-06
NEGATIVE = -1000000000.0
HIGHEST = lax.Precision.HIGHEST

@jax.custom_vjp
def low(v):
    return lax.optimization_barrier(v.astype(jnp.bfloat16)).astype(jnp.float32)

@jax.custom_vjp
def low_back(v):
    return v

def low_keep(v):
    return (low(v), None)

def low_pass(kept, grad):
    return (grad,)

def back_keep(v):
    return (v, None)

def back_low(kept, grad):
    return (low(grad),)
low.defvjp(low_keep, low_pass)
low_back.defvjp(back_keep, back_low)

def round_both(value):
    return low(low_back(value))

def product(left, right):
    return jnp.dot(left, right, precision=HIGHEST, preferred_element_type=jnp.float32)

def norm_apply(value, gain):
    return value * lax.rsqrt(lax.optimization_barrier(jnp.mean(value * value, axis=-1, keepdims=True)) + EPSILON) * gain

def layout(lengths):
    index = jnp.arange(GTOK, dtype=jnp.int32)
    after = index - PROMPT
    bounds = jnp.cumsum(lengths).astype(jnp.int32)
    member = lax.optimization_barrier(jnp.sum((after[:, None] >= bounds[None, :]).astype(jnp.int32), axis=1)).astype(jnp.int32)
    earlier = lax.optimization_barrier(jnp.sum(jnp.where(jnp.arange(CONT, dtype=jnp.int32)[None, :] < member[:, None], lengths[None, :], 0), axis=1)).astype(jnp.int32)
    position = jnp.where(index < PROMPT, index, PROMPT + after - earlier).astype(jnp.int32)
    segment = jnp.where(index < PROMPT, 0, member + 1).astype(jnp.int32)
    allowed = (position[None, :] <= position[:, None]) & ((segment[None, :] == 0) | (segment[None, :] == segment[:, None]))
    return (position, allowed)

def attend(queries, key_rows, value_rows, extra, allowed):
    scores = jnp.einsum('qhd,khd->qhk', queries, key_rows, precision=HIGHEST)
    if extra is not None:
        scores = scores + extra
    scores = low_back(scores)
    if allowed is not None:
        scores = jnp.where(allowed[:, None, :], scores, NEGATIVE)
    probs = jax.nn.softmax(scores, axis=-1)
    context = jnp.einsum('qhk,khd->qhd', low(probs), value_rows, precision=HIGHEST)
    return round_both(context.reshape(context.shape[0], INNER))

def group_forward(params, item, buckets):
    qkv_weight, self_weight, cross_q_weight, cross_kv_weight, cross_weight, in_weight, out_weight, gain_one, gain_two, gain_three, bias_rows = params
    inputs, encoded, lengths = item
    position, allowed = layout(lengths)
    distance = jnp.clip(position[:, None] - position[None, :], 0, DIST - 1).astype(jnp.int32)
    chosen = jnp.take(buckets, distance, axis=0)
    score_bias = jnp.transpose(jnp.take(bias_rows, chosen, axis=0), (0, 2, 1))
    normed = low(norm_apply(inputs, gain_one))
    joined = round_both(product(normed, qkv_weight))
    queries = joined[:, :INNER].reshape(GTOK, HEADS, DK)
    key_rows = joined[:, INNER:2 * INNER].reshape(GTOK, HEADS, DK)
    value_rows = joined[:, 2 * INNER:].reshape(GTOK, HEADS, DK)
    context = attend(queries, key_rows, value_rows, score_bias, allowed)
    first = inputs + low_back(product(context, self_weight))
    normed_two = low(norm_apply(first, gain_two))
    cross_queries = round_both(product(normed_two, cross_q_weight)).reshape(GTOK, HEADS, DK)
    cross_joined = round_both(product(encoded, cross_kv_weight))
    cross_keys = cross_joined[:, :INNER].reshape(ENC, HEADS, DK)
    cross_values = cross_joined[:, INNER:].reshape(ENC, HEADS, DK)
    cross_context = attend(cross_queries, cross_keys, cross_values, None, None)
    second = first + low_back(product(cross_context, cross_weight))
    normed_three = low(norm_apply(second, gain_three))
    gate_up = low_back(product(normed_three, in_weight))
    hidden = low(jax.nn.gelu(gate_up[:, :FF], approximate=True) * gate_up[:, FF:])
    return second + low_back(product(hidden, out_weight))

def reference(dec_in, enc_out, d_out, cont_len, buckets, self_qkv, self_out, cross_q, cross_kv, cross_out, ff_in, ff_out, gain_self, gain_cross, gain_ff, rel_bias):
    params = (self_qkv.astype(jnp.float32), self_out.astype(jnp.float32), cross_q.astype(jnp.float32), cross_kv.astype(jnp.float32), cross_out.astype(jnp.float32), ff_in.astype(jnp.float32), ff_out.astype(jnp.float32), gain_self.astype(jnp.float32), gain_cross.astype(jnp.float32), gain_ff.astype(jnp.float32), rel_bias.astype(jnp.float32))
    inputs = dec_in.astype(jnp.float32)
    encoded = enc_out.astype(jnp.float32)
    step_fn = jax.checkpoint(partial(group_forward, buckets=buckets))

    def whole_layer(inputs, encoded, params):
        return lax.map(lambda item: step_fn(params, item), (inputs, encoded, cont_len))
    output, pullback = jax.vjp(whole_layer, inputs, encoded, params)
    grad_inputs, grad_encoded, grad_params = pullback(d_out.astype(jnp.float32))
    return (output.astype(jnp.bfloat16), grad_inputs.astype(jnp.bfloat16), grad_encoded.astype(jnp.bfloat16), grad_params[0], grad_params[1], grad_params[2], grad_params[3], grad_params[4], grad_params[5], grad_params[6], grad_params[7], grad_params[8], grad_params[9], grad_params[10])
```

```python
import functools

import jax
import jax.numpy as jnp
from jax import lax
from jax.experimental import pallas as pl
from jax.experimental.pallas import tpu as pltpu
from jax.sharding import PartitionSpec as P

EPSILON = 1e-06
NEGATIVE = -1000000000.0

MESH = pl.DeviceIdType.MESH


class Place:
    def __init__(self):
        self.d = lax.axis_index("dp")
        fs = lax.axis_index("fsdp")
        self.z = fs // 2
        self.c = fs % 2
        self.far = self.z // 2
        self.near = self.z * (1 - self.far) + (3 - self.z) * self.far
        self.dx = self.d + 1 - 2 * (self.d % 2)
        self.dy = (self.d + 2) % 4
        self.dd = 3 - self.d

    def at(self, d, z, c):
        return (d, z * 2 + c)

    def order(self, j):
        s = (self.near, 1 - self.near, 2, 3)[j]
        return s * (1 - self.far) + (3 - s) * self.far

    def sides(self, zp):
        odd = zp % 2
        first = self.dy * (1 - odd) + self.dx * odd
        second = self.dx * (1 - odd) + self.dy * odd
        return first, second


def greet(p):
    barrier = pltpu.get_barrier_semaphore()

    def hello(device):
        pl.semaphore_signal(barrier, inc=1, device_id=device, device_id_type=MESH)

    hello(p.at(p.dx, p.z, p.c))
    hello(p.at(p.dy, p.z, p.c))
    hello(p.at(p.d, p.z, 1 - p.c))

    @pl.when(p.z > 0)
    def _():
        hello(p.at(p.d, p.z - 1, p.c))

    @pl.when(p.z < 3)
    def _():
        hello(p.at(p.d, p.z + 1, p.c))

    pl.semaphore_wait(barrier, 3 + (p.z + 2) // 3 + (5 - p.z) // 3)


def gather_kernel(groups, count, *refs):
    own = refs[:count]
    out = refs[count : 2 * count]
    recv, sent, local = refs[2 * count :]
    p = Place()
    d, z, c = p.d, p.z, p.c

    for i in range(count):
        pltpu.make_async_copy(own[i], out[i].at[d, z, c], local.at[i]).start()

    greet(p)

    def copy(i, j, kind, dd, zp, target, mine=False):
        return pltpu.make_async_remote_copy(
            src_ref=own[i] if mine else out[i].at[dd, zp, c],
            dst_ref=out[i].at[dd, zp, c],
            send_sem=sent.at[i, j, kind],
            recv_sem=recv.at[i, dd, zp, c],
            device_id=target,
            device_id_type=MESH,
        )

    def arrived(i, dd, zp, cc):
        pltpu.make_async_remote_copy(
            src_ref=out[i].at[dd, zp, cc],
            dst_ref=out[i].at[dd, zp, cc],
            send_sem=sent.at[i, 0, 0],
            recv_sem=recv.at[i, dd, zp, cc],
            device_id=p.at(d, z, 1 - c),
            device_id_type=MESH,
        ).wait_recv()

    def along(i, j, act):
        zp = p.order(j)
        mine = j == 0

        @pl.when((zp <= z) & (z < 3))
        def _():
            act(copy(i, j, 0, d, zp, p.at(d, z + 1, c), mine))

        @pl.when((zp >= z) & (z > 0))
        def _():
            act(copy(i, j, 1, d, zp, p.at(d, z - 1, c), mine))

    def across(i, j, act):
        zp = p.order(j)
        mine = j == 0
        act(copy(i, j, 2, d, zp, p.at(p.dx, z, c), mine))
        act(copy(i, j, 3, d, zp, p.at(p.dy, z, c), mine))
        act(copy(i, j, 4, d, zp, p.at(d, z, 1 - c), mine))

    def onward(i, j, act):
        zp = p.order(j)
        first, second = p.sides(zp)
        act(copy(i, j, 5, second, zp, p.at(first, z, c)))
        act(copy(i, j, 6, second, zp, p.at(d, z, 1 - c)))
        act(copy(i, j, 7, first, zp, p.at(d, z, 1 - c)))

    def last(i, j, act):
        zp = p.order(j)
        act(copy(i, j, 8, p.dd, zp, p.at(d, z, 1 - c)))

    start = lambda cp: cp.start()
    done = lambda cp: cp.wait_send()
    steps = [(g, j) for g in groups for j in range(4)]
    for n in range(len(steps) + 2):
        if n < len(steps):
            g, j = steps[n]
            for i in g:
                if j > 0:
                    arrived(i, d, p.order(j), c)
                along(i, j, start)
                across(i, j, start)
        if 1 <= n <= len(steps):
            g, j = steps[n - 1]
            for i in g:
                zp = p.order(j)
                first, second = p.sides(zp)
                arrived(i, second, zp, c)
                arrived(i, first, zp, c)
                onward(i, j, start)
        if n >= 2:
            g, j = steps[n - 2]
            for i in g:
                arrived(i, p.dd, p.order(j), c)
                last(i, j, start)
    for g, j in steps:
        for i in g:
            for dd in range(4):
                arrived(i, dd, p.order(j), 1 - c)
            along(i, j, done)
            across(i, j, done)
            onward(i, j, done)
            last(i, j, done)
    for i in range(count):
        pltpu.make_async_copy(own[i], out[i].at[d, z, c], local.at[i]).wait()


def gather_all(shards, groups):
    count = len(shards)
    return pl.pallas_call(
        functools.partial(gather_kernel, groups, count),
        out_shape=[jax.ShapeDtypeStruct((4, 4, 2) + s.shape, s.dtype) for s in shards],
        in_specs=[pl.BlockSpec(memory_space=pltpu.VMEM)] * count,
        out_specs=[pl.BlockSpec(memory_space=pl.ANY)] * count,
        scratch_shapes=[
            pltpu.SemaphoreType.DMA((count, 4, 4, 2)),
            pltpu.SemaphoreType.DMA((count, 4, 9)),
            pltpu.SemaphoreType.DMA((count,)),
        ],
        compiler_params=pltpu.CompilerParams(collective_id=1, has_side_effects=True),
    )(*shards)


def reduce_kernel(groups, count, *refs):
    part = refs[:count]
    out = refs[count : 2 * count]
    land_core = refs[2 * count : 3 * count]
    land = refs[3 * count : 4 * count]
    stage = refs[4 * count : 5 * count]
    total = refs[5 * count : 6 * count]
    core_send, core_recv, send, recv, load, store = refs[6 * count :]
    p = Place()
    d, z, c = p.d, p.z, p.c
    greet(p)
    steps = [(g, j) for g in groups for j in (3, 2, 1, 0)]

    def core_copy(i, dd, zp):
        return pltpu.make_async_remote_copy(
            src_ref=part[i].at[dd, zp, 1 - c],
            dst_ref=land_core[i].at[dd, zp],
            send_sem=core_send.at[i, dd, zp],
            recv_sem=core_recv.at[i, dd, zp],
            device_id=p.at(d, z, 1 - c),
            device_id_type=MESH,
        )

    def over(i, kind, zp, target):
        return pltpu.make_async_remote_copy(
            src_ref=total[i].at[min(kind, 3)],
            dst_ref=land[i].at[kind, zp],
            send_sem=send.at[i, min(kind, 3)],
            recv_sem=recv.at[i, kind, zp],
            device_id=target,
            device_id_type=MESH,
        )

    def add_into(i, slot, sources, keep=False):
        for s, src in enumerate(sources):
            pltpu.make_async_copy(src, stage[i].at[s], load.at[i, s]).start()
        for s, src in enumerate(sources):
            pltpu.make_async_copy(src, stage[i].at[s], load.at[i, s]).wait()
        rows = stage[i].shape[1]

        def body(r, carry):
            at = pl.ds(pl.multiple_of(r * 8, 8), 8)
            value = total[i][slot, at, :].astype(jnp.float32) if keep else None
            for s in range(len(sources)):
                more = stage[i][s, at, :].astype(jnp.float32)
                value = more if value is None else value + more
            total[i][slot, at, :] = value.astype(jnp.bfloat16)
            return carry

        lax.fori_loop(0, rows // 8, body, 0)

    def free(i, slot, n, first):
        if n > first:
            over(i, slot, 0, p.at(d, z, 1 - c)).wait_send()

    for g, j in steps:
        for i in g:
            for dd in range(4):
                core_copy(i, dd, p.order(j)).start()

    seen = {}

    def stage_one(i, j):
        zp = p.order(j)
        first, second = p.sides(zp)
        for dd in range(4):
            core_copy(i, dd, zp).wait_recv()
        for slot, chunk in ((0, p.dd), (1, first)):
            if seen.get((i, slot)):
                over(i, slot, 0, p.at(first, z, c)).wait_send()
            seen[(i, slot)] = True
            add_into(i, slot, [part[i].at[chunk, zp, c], land_core[i].at[chunk, zp]])
            over(i, slot, zp, p.at(first, z, c)).start()

    def stage_two(i, j):
        zp = p.order(j)
        first, second = p.sides(zp)
        over(i, 0, zp, p.at(first, z, c)).wait_recv()
        if seen.get((i, 2)):
            over(i, 2, 0, p.at(first, z, c)).wait_send()
        seen[(i, 2)] = True
        add_into(i, 2, [part[i].at[second, zp, c], land_core[i].at[second, zp], land[i].at[0, zp]])
        over(i, 2, zp, p.at(second, z, c)).start()

    def stage_three(i, j):
        zp = p.order(j)
        first, second = p.sides(zp)
        over(i, 1, zp, p.at(first, z, c)).wait_recv()
        over(i, 2, zp, p.at(first, z, c)).wait_recv()
        if seen.get((i, 3)):
            over(i, 3, 0, p.at(first, z, c)).wait_send()
        seen[(i, 3)] = j > 0
        add_into(i, 3, [part[i].at[d, zp, c], land_core[i].at[d, zp], land[i].at[1, zp], land[i].at[2, zp]])

        @pl.when((zp >= z) & (z > 0))
        def _():
            over(i, 3, zp, p.at(first, z, c)).wait_recv()
            add_into(i, 3, [land[i].at[3, zp]], keep=True)

        @pl.when((zp <= z) & (z < 3))
        def _():
            over(i, 4, zp, p.at(first, z, c)).wait_recv()
            add_into(i, 3, [land[i].at[4, zp]], keep=True)

        if j > 0:

            @pl.when(zp > z)
            def _():
                over(i, 3, zp, p.at(d, z + 1, c)).start()

            @pl.when(zp < z)
            def _():
                over(i, 4, zp, p.at(d, z - 1, c)).start()

        else:
            keep = pltpu.make_async_copy(total[i].at[3], out[i], store.at[i])
            keep.start()
            keep.wait()

    for n in range(len(steps) + 2):
        if n < len(steps):
            g, j = steps[n]
            for i in g:
                stage_one(i, j)
        if 1 <= n <= len(steps):
            g, j = steps[n - 1]
            for i in g:
                stage_two(i, j)
        if n >= 2:
            g, j = steps[n - 2]
            for i in g:
                stage_three(i, j)
    for g, j in steps:
        for i in g:
            for dd in range(4):
                core_copy(i, dd, p.order(j)).wait_send()
    for g in groups:
        for i in g:
            for slot in range(3):
                over(i, slot, 0, p.at(p.dx, z, c)).wait_send()


def reduce_all(parts, groups):
    count = len(parts)
    blocks = [s.shape[3:] for s in parts]
    bf = jnp.bfloat16
    outs = pl.pallas_call(
        functools.partial(reduce_kernel, groups, count),
        out_shape=[jax.ShapeDtypeStruct(b, bf) for b in blocks]
        + [jax.ShapeDtypeStruct((4, 4) + b, bf) for b in blocks]
        + [jax.ShapeDtypeStruct((5, 4) + b, bf) for b in blocks],
        in_specs=[pl.BlockSpec(memory_space=pl.ANY)] * count,
        out_specs=[pl.BlockSpec(memory_space=pl.ANY)] * (3 * count),
        scratch_shapes=[pltpu.VMEM((4,) + b, bf) for b in blocks]
        + [pltpu.VMEM((4,) + b, bf) for b in blocks]
        + [
            pltpu.SemaphoreType.DMA((count, 4, 4)),
            pltpu.SemaphoreType.DMA((count, 4, 4)),
            pltpu.SemaphoreType.DMA((count, 4)),
            pltpu.SemaphoreType.DMA((count, 5, 4)),
            pltpu.SemaphoreType.DMA((count, 4)),
            pltpu.SemaphoreType.DMA((count,)),
        ],
        compiler_params=pltpu.CompilerParams(collective_id=2, has_side_effects=True),
    )(*parts)
    return outs[:count]


F32 = jnp.float32
BF16 = jnp.bfloat16
TILE = 128
FF_TILE = 256
HIGH = 64 * 1024 * 1024 - 65536


def mm(a, b):
    return lax.dot_general(a, b, (((1,), (0,)), ((), ())), preferred_element_type=F32)


def mm_nt(a, b):
    return lax.dot_general(a, b, (((1,), (1,)), ((), ())), preferred_element_type=F32)


def mm_tn(a, b):
    return lax.dot_general(a, b, (((0,), (0,)), ((), ())), preferred_element_type=F32)


def inverse_rms(value):
    return lax.rsqrt(jnp.mean(value * value, axis=-1, keepdims=True) + EPSILON)


def norm_back(value, gain, upstream):
    inverse = inverse_rms(value)
    unit = value * inverse
    scaled = upstream * gain
    mean = jnp.mean(scaled * unit, axis=-1, keepdims=True)
    return inverse * (scaled - unit * mean), jnp.sum(upstream * unit, axis=0, keepdims=True)


def side_by_side(pieces):
    return jnp.concatenate(pieces, axis=1)


def toeplitz(row):
    wide = jnp.broadcast_to(row, (TILE, 2 * TILE))
    return pltpu.roll(wide, 0, 1, stride=1, stride_axis=0)[:, :TILE]


def diagonal_sums(block):
    wide = side_by_side([block, jnp.zeros_like(block)])
    return jnp.sum(pltpu.roll(wide, 0, 1, stride=1, stride_axis=0), axis=0, keepdims=True)


def softmax_rows(scores):
    highest = jnp.max(scores, axis=-1, keepdims=True)
    shifted = jnp.exp(scores - highest)
    return shifted / jnp.sum(shifted, axis=-1, keepdims=True)


def self_probs(queries, keys, bias, qi, first_length):
    scores = mm_nt(queries, keys)
    row = lax.broadcasted_iota(jnp.int32, (TILE, TILE), 0)
    column = lax.broadcasted_iota(jnp.int32, (TILE, TILE), 1)
    keep = column <= row
    if qi < 2:
        pieces = [toeplitz(bias[qi - kj]) for kj in range(qi + 1)]
    else:
        second = row >= first_length
        pieces = [
            jnp.where(second, toeplitz(bias[3]), toeplitz(bias[2])),
            jnp.where(second, toeplitz(bias[4]), toeplitz(bias[1])),
            toeplitz(bias[0]),
        ]
        keep = keep & (second == (column >= first_length))
    scores = scores + side_by_side(pieces)
    last = jnp.where(keep, scores[:, qi * TILE :], NEGATIVE)
    scores = last if qi == 0 else side_by_side([scores[:, : qi * TILE], last])
    return softmax_rows(scores)


def head_of(array, head, size):
    return array[:, head * size : (head + 1) * size]


def before_kernel(
    heads, lengths, x_ref, enc_ref, gains, wide, tall, table,
    joined_ref, context_ref, first_ref, crossq_ref, crossj_ref, crossc_ref, second_ref,
):
    first_length = lengths[pl.program_id(0), 0]
    inner = context_ref.shape[2]
    size = inner // heads
    blocks = wide.shape[0]
    qkv_width = 3 * inner // blocks
    q_width = inner // blocks
    half = tall.shape[2] // 2
    x = x_ref[0].astype(F32)
    normed = (x * inverse_rms(x) * gains[0:1]).astype(BF16)
    joined = side_by_side([mm(normed, wide[b, :, :qkv_width]) for b in range(blocks)]).astype(BF16)
    joined_ref[0] = joined
    queries, keys, values = joined[:, :inner], joined[:, inner : 2 * inner], joined[:, 2 * inner :]
    contexts = []
    for h in range(heads):
        q, k, v = head_of(queries, h, size), head_of(keys, h, size), head_of(values, h, size)
        bias = [table[0, n, h : h + 1, :] for n in range(5)]
        rows = []
        for qi in range(3):
            upto = (qi + 1) * TILE
            probs = self_probs(q[qi * TILE : upto], k[:upto], bias, qi, first_length)
            rows.append(mm(probs.astype(BF16), v[:upto]))
        contexts.append(jnp.concatenate(rows, axis=0))
    context = side_by_side(contexts).astype(BF16)
    context_ref[0] = context
    flat = lambda part: part.reshape(inner, part.shape[2])
    first = x + side_by_side([mm(context, flat(tall[b, :, :half])) for b in range(blocks)])
    first_ref[0] = first
    normed_two = (first * inverse_rms(first) * gains[1:2]).astype(BF16)
    crossq = side_by_side(
        [mm(normed_two, wide[b, :, qkv_width : qkv_width + q_width]) for b in range(blocks)]
    ).astype(BF16)
    crossq_ref[0] = crossq
    crossj = side_by_side([mm(enc_ref[0], wide[b, :, qkv_width + q_width :]) for b in range(blocks)]).astype(BF16)
    crossj_ref[0] = crossj
    contexts = []
    for h in range(heads):
        q, k, v = head_of(crossq, h, size), head_of(crossj, h, size), head_of(crossj, heads + h, size)
        probs = softmax_rows(mm_nt(q, k))
        contexts.append(mm(probs.astype(BF16), v))
    crossc = side_by_side(contexts).astype(BF16)
    crossc_ref[0] = crossc
    second_ref[0] = first + side_by_side([mm(crossc, flat(tall[b, :, half:])) for b in range(blocks)])


def one(shape, index):
    return pl.BlockSpec(shape, index)


def fixed(array):
    rank = array.ndim
    return pl.BlockSpec(array.shape, lambda *_: (0,) * rank, pipeline_mode=pl.Buffered(1))


def per_group(array):
    rest = array.shape[1:]
    return pl.BlockSpec((1,) + tuple(rest), lambda g: (g,) + (0,) * len(rest))


def before(lengths, x, enc, gains, wide, tall, table, heads):
    groups, tokens, width = x.shape
    inner = tall.shape[1] * tall.shape[2] // 2
    outs = [
        jax.ShapeDtypeStruct((groups, tokens, 3 * inner), BF16),
        jax.ShapeDtypeStruct((groups, tokens, inner), BF16),
        jax.ShapeDtypeStruct((groups, tokens, width), F32),
        jax.ShapeDtypeStruct((groups, tokens, inner), BF16),
        jax.ShapeDtypeStruct((groups, enc.shape[1], 2 * inner), BF16),
        jax.ShapeDtypeStruct((groups, tokens, inner), BF16),
        jax.ShapeDtypeStruct((groups, tokens, width), F32),
    ]
    return pl.pallas_call(
        functools.partial(before_kernel, heads),
        grid=(groups,),
        out_shape=outs,
        in_specs=[
            pl.BlockSpec(memory_space=pltpu.SMEM),
            per_group(x),
            per_group(enc),
            fixed(gains),
            fixed(wide),
            fixed(tall),
            per_group(table),
        ],
        out_specs=[per_group(o) for o in outs],
        compiler_params=pltpu.CompilerParams(vmem_limit_bytes=HIGH),
    )(lengths, x, enc, gains, wide, tall, table)


def feed_kernel(second_ref, upstream_ref, gains, wi_ref, wo_ref, out_ref, three_ref, dwi_ref, dwo_ref, normed, flipped, acc):
    step = pl.program_id(0) * pl.num_programs(1) + pl.program_id(1)
    last = pl.num_programs(0) * pl.num_programs(1) - 1
    upstream = upstream_ref[...]

    @pl.when(step == 0)
    def _():
        second = second_ref[...]
        value = (second * inverse_rms(second) * gains[2:3]).astype(BF16)
        normed[...] = value
        flipped[...] = value.T
        acc[...] = second
        three_ref[...] = jnp.zeros_like(three_ref)

    blocks = wo_ref.shape[0]
    wg, wu = wi_ref[0, 0], wi_ref[1, 0]
    wo = side_by_side([wo_ref[b] for b in range(blocks)])
    gate, up = mm(normed[...], wg), mm(normed[...], wu)
    grad_hidden = mm_nt(upstream, wo)
    root = 0.7978845608028654
    square = gate * gate
    tanh = jnp.tanh(root * gate * (1.0 + 0.044715 * square))
    half = 0.5 * (1.0 + tanh)
    gelu = gate * half
    slope = half + 0.5 * gate * (1.0 - tanh * tanh) * (root * (1.0 + 3 * 0.044715 * square))
    hidden = (gelu * up).astype(BF16)
    grad_gate = (slope * up * grad_hidden).astype(BF16)
    grad_up = (gelu * grad_hidden).astype(BF16)
    acc[...] += mm(hidden, wo)
    dwo = mm_tn(hidden, upstream).astype(BF16)
    columns = wo_ref.shape[2]
    for b in range(blocks):
        dwo_ref[b] = dwo[:, b * columns : (b + 1) * columns]
    dwi_ref[0, 0] = mm(flipped[...], grad_gate).astype(BF16)
    dwi_ref[1, 0] = mm(flipped[...], grad_up).astype(BF16)
    three_ref[...] += mm_nt(grad_gate, wg) + mm_nt(grad_up, wu)

    @pl.when(step == last)
    def _():
        out_ref[...] = acc[...].astype(BF16)


def feed(second, upstream, gains, wi, wo):
    tokens, width = second.shape
    blocks, units, columns = wo.shape
    wi = wi.reshape(2, blocks // 2, width, wi.shape[2])
    tiles = wi.shape[3] // FF_TILE
    wi_spec = pl.BlockSpec((2, 1, width, FF_TILE), lambda d, s: (0, d, 0, s))
    wo_spec = pl.BlockSpec((blocks, FF_TILE, columns), lambda d, s: (0, d * tiles + s, 0))
    whole = pl.BlockSpec((tokens, width), lambda d, s: (0, 0), pipeline_mode=pl.Buffered(1))
    out, three, dwi, dwo = pl.pallas_call(
        feed_kernel,
        grid=(blocks // 2, tiles),
        out_shape=[
            jax.ShapeDtypeStruct((tokens, width), BF16),
            jax.ShapeDtypeStruct((tokens, width), F32),
            jax.ShapeDtypeStruct(wi.shape, BF16),
            jax.ShapeDtypeStruct(wo.shape, BF16),
        ],
        in_specs=[whole, whole, fixed(gains), wi_spec, wo_spec],
        out_specs=[whole, whole, wi_spec, wo_spec],
        scratch_shapes=[
            pltpu.VMEM((tokens, width), BF16),
            pltpu.VMEM((width, tokens), BF16),
            pltpu.VMEM((tokens, width), F32),
        ],
        compiler_params=pltpu.CompilerParams(vmem_limit_bytes=HIGH),
    )(second, upstream, gains, wi, wo)
    return out, three, dwi.reshape(blocks, width, -1), dwo


def after_kernel(
    heads, lengths, x_ref, enc_ref, gains, wide, tall, table,
    joined_ref, context_ref, first_ref, crossq_ref, crossj_ref, crossc_ref, second_ref, upstream_ref, three_ref,
    ddec_ref, denc_ref, dgain_ref, dtable_ref,
    normed_ref, normed_two_ref, cross_branch_ref, self_branch_ref, gjoined_ref, gcrossq_ref, gcrossj_ref,
):
    g = pl.program_id(0)
    first_length = lengths[g, 0]
    inner = context_ref.shape[2]
    size = inner // heads
    blocks = wide.shape[0]
    qkv_width = 3 * inner // blocks
    q_width = inner // blocks
    half = tall.shape[2] // 2
    flat = lambda part: part.reshape(inner, part.shape[2])
    bcol = lambda array, b, w: array[:, b * w : (b + 1) * w]

    second = second_ref[0]
    part, gain_three = norm_back(second, gains[2:3], three_ref[0])
    grad_second = upstream_ref[0].astype(F32) + part
    cross_branch = grad_second.astype(BF16)
    cross_branch_ref[0] = cross_branch
    gctx = mm_nt(cross_branch, side_by_side([flat(tall[b, :, half:]) for b in range(blocks)])).astype(BF16)
    crossq, crossj = crossq_ref[0], crossj_ref[0]
    gq, gk, gv = [], [], []
    for h in range(heads):
        q, k, v = head_of(crossq, h, size), head_of(crossj, h, size), head_of(crossj, heads + h, size)
        u = head_of(gctx, h, size)
        probs = softmax_rows(mm_nt(q, k))
        gv.append(mm_tn(probs.astype(BF16), u))
        gp = mm_nt(u, v)
        ds = (probs * (gp - jnp.sum(gp * probs, axis=-1, keepdims=True))).astype(BF16)
        gq.append(mm(ds, k))
        gk.append(mm_tn(ds, q))
    gcrossq = side_by_side(gq).astype(BF16)
    gcrossj = side_by_side(gk + gv).astype(BF16)
    gcrossq_ref[0] = gcrossq
    gcrossj_ref[0] = gcrossj
    grad_two = mm_nt(bcol(gcrossq, 0, q_width), wide[0, :, qkv_width : qkv_width + q_width])
    denc = mm_nt(bcol(gcrossj, 0, 2 * q_width), wide[0, :, qkv_width + q_width :])
    for b in range(1, blocks):
        grad_two += mm_nt(bcol(gcrossq, b, q_width), wide[b, :, qkv_width : qkv_width + q_width])
        denc += mm_nt(bcol(gcrossj, b, 2 * q_width), wide[b, :, qkv_width + q_width :])
    denc_ref[0] = denc.astype(BF16)
    first = first_ref[0]
    normed_two_ref[0] = (first * inverse_rms(first) * gains[1:2]).astype(BF16)
    part, gain_two = norm_back(first, gains[1:2], grad_two)
    grad_first = grad_second + part
    self_branch = grad_first.astype(BF16)
    self_branch_ref[0] = self_branch
    gctx = mm_nt(self_branch, side_by_side([flat(tall[b, :, :half]) for b in range(blocks)])).astype(BF16)
    joined = joined_ref[0]
    queries, keys, values = joined[:, :inner], joined[:, inner : 2 * inner], joined[:, 2 * inner :]
    row = lax.broadcasted_iota(jnp.int32, (TILE, TILE), 0)
    column = lax.broadcasted_iota(jnp.int32, (TILE, TILE), 1)
    turn = jnp.where(row + column == TILE - 1, 1.0, 0.0).astype(BF16)
    late = row >= first_length
    late_turned = (TILE - 1 - row) >= first_length
    gq, gk, gv, sums = [], [], [], []
    for h in range(heads):
        q, k, v = head_of(queries, h, size), head_of(keys, h, size), head_of(values, h, size)
        u = head_of(gctx, h, size)
        bias = [table[0, n, h : h + 1, :] for n in range(5)]
        hq = []
        hk = [None] * 3
        hv = [None] * 3
        diag = {}
        for qi in range(3):
            upto = (qi + 1) * TILE
            at = slice(qi * TILE, upto)
            probs = self_probs(q[at], k[:upto], bias, qi, first_length)
            pv = mm_tn(probs.astype(BF16), u[at])
            gp = mm_nt(u[at], v[:upto])
            ds = (probs * (gp - jnp.sum(gp * probs, axis=-1, keepdims=True))).astype(BF16)
            hq.append(mm(ds, k[:upto]))
            pk = mm_tn(ds, q[at])
            turned = mm(turn, ds)
            for kj in range(qi + 1):
                s = slice(kj * TILE, (kj + 1) * TILE)
                hv[kj] = pv[s] if hv[kj] is None else hv[kj] + pv[s]
                hk[kj] = pk[s] if hk[kj] is None else hk[kj] + pk[s]
                piece = turned[:, s]
                if qi == 2 and kj < 2:
                    diag[3 + kj] = jnp.where(late_turned, piece, 0.0)
                    piece = jnp.where(late_turned, 0.0, piece)
                n = qi - kj
                diag[n] = piece if n not in diag else diag[n] + piece
        gq.append(jnp.concatenate(hq, axis=0))
        gk.append(jnp.concatenate(hk, axis=0))
        gv.append(jnp.concatenate(hv, axis=0))
        for n in range(5):
            dtable_ref[0, n, h : h + 1, :] = diagonal_sums(diag[n])
    for n in range(5):
        dtable_ref[0, n, heads:, :] = jnp.zeros((dtable_ref.shape[2] - heads, 2 * TILE), F32)
    gjoined = side_by_side(gq + gk + gv).astype(BF16)
    gjoined_ref[0] = gjoined
    grad_one = mm_nt(bcol(gjoined, 0, qkv_width), wide[0, :, :qkv_width])
    for b in range(1, blocks):
        grad_one += mm_nt(bcol(gjoined, b, qkv_width), wide[b, :, :qkv_width])
    x = x_ref[0].astype(F32)
    normed_ref[0] = (x * inverse_rms(x) * gains[0:1]).astype(BF16)
    part, gain_one = norm_back(x, gains[0:1], grad_one)
    ddec_ref[0] = (grad_first + part).astype(BF16)
    dgain_ref[0, 0:1] = gain_one
    dgain_ref[0, 1:2] = gain_two
    dgain_ref[0, 2:3] = gain_three
    dgain_ref[0, 3:] = jnp.zeros((5, x.shape[1]), F32)


def weights_kernel(
    qkv_width, q_width, enc, context, crossc, normed, normed_two, cross_branch, self_branch, gjoined, gcrossq, gcrossj,
    dwide, dtall,
):
    blocks = dwide.shape[0]
    half, columns = dtall.shape[2] // 2, dtall.shape[3]
    bcol = lambda array, b, w: array[:, b * w : (b + 1) * w]
    for b in range(blocks):
        dwide[b, :, :qkv_width] = mm_tn(normed[...], bcol(gjoined, b, qkv_width)).astype(BF16)
        dwide[b, :, qkv_width : qkv_width + q_width] = mm_tn(normed_two[...], bcol(gcrossq, b, q_width)).astype(BF16)
        dwide[b, :, qkv_width + q_width :] = mm_tn(enc[...], bcol(gcrossj, b, 2 * q_width)).astype(BF16)
        part = mm_tn(context[...], bcol(self_branch, b, columns)).astype(BF16)
        dtall[b, :, :half] = part.reshape(-1, half, columns)
        part = mm_tn(crossc[...], bcol(cross_branch, b, columns)).astype(BF16)
        dtall[b, :, half:] = part.reshape(-1, half, columns)


def weights(enc, context, crossc, factors, wide, tall):
    flat = lambda array: array.reshape(-1, array.shape[2])
    args = [flat(a) for a in (enc, context, crossc, *factors)]
    q_width = context.shape[2] // wide.shape[0]
    return pl.pallas_call(
        functools.partial(weights_kernel, 3 * q_width, q_width),
        out_shape=[jax.ShapeDtypeStruct(wide.shape, BF16), jax.ShapeDtypeStruct(tall.shape, BF16)],
        compiler_params=pltpu.CompilerParams(vmem_limit_bytes=HIGH),
    )(*args)


def after(lengths, x, enc, gains, wide, tall, table, saved, upstream, three, heads):
    groups, tokens, width = x.shape
    joined, context, first, crossq, crossj, crossc, second = saved
    outs = [
        jax.ShapeDtypeStruct(x.shape, BF16),
        jax.ShapeDtypeStruct(enc.shape, BF16),
        jax.ShapeDtypeStruct((groups, 8, width), F32),
        jax.ShapeDtypeStruct(table.shape, F32),
        jax.ShapeDtypeStruct(x.shape, BF16),
        jax.ShapeDtypeStruct(x.shape, BF16),
        jax.ShapeDtypeStruct(x.shape, BF16),
        jax.ShapeDtypeStruct(x.shape, BF16),
        jax.ShapeDtypeStruct(joined.shape, BF16),
        jax.ShapeDtypeStruct(crossq.shape, BF16),
        jax.ShapeDtypeStruct(crossj.shape, BF16),
    ]
    grouped = [joined, context, first, crossq, crossj, crossc, second, upstream, three]
    return pl.pallas_call(
        functools.partial(after_kernel, heads),
        grid=(groups,),
        out_shape=outs,
        in_specs=[
            pl.BlockSpec(memory_space=pltpu.SMEM),
            per_group(x),
            per_group(enc),
            fixed(gains),
            fixed(wide),
            fixed(tall),
            per_group(table),
        ]
        + [per_group(a) for a in grouped],
        out_specs=[per_group(o) for o in outs],
        compiler_params=pltpu.CompilerParams(vmem_limit_bytes=HIGH),
    )(lengths, x, enc, gains, wide, tall, table, *grouped)


def table_distances(lengths, turned):
    starts = jnp.array([0, TILE, 2 * TILE, 2 * TILE, TILE], jnp.int32)
    moved = jnp.array([0, 0, 0, 1, 1], jnp.int32)
    start = starts[None, :] - moved[None, :] * lengths[:, :1]
    index = jnp.arange(2 * TILE, dtype=jnp.int32)
    if turned:
        offset = TILE - 1 - index
    else:
        offset = -jnp.where(index < TILE, index, index - 2 * TILE)
    return start[:, :, None] + offset[None, None, :]


def distance_onehot(lengths, turned, count):
    distance = jnp.clip(table_distances(lengths, turned), 0, count - 1)
    return distance[..., None] == jnp.arange(count, dtype=jnp.int32)


def bias_tables(lengths, buckets, bias_rows):
    count = buckets.shape[0]
    labels = (buckets[:, None] == jnp.arange(bias_rows.shape[0], dtype=jnp.int32)).astype(BF16)
    by_distance = jnp.dot(labels, bias_rows, preferred_element_type=F32).astype(BF16)
    by_distance = jnp.pad(by_distance, ((0, 0), (0, 8 - bias_rows.shape[1])))
    onehot = distance_onehot(lengths, False, count).astype(BF16)
    return jnp.einsum("gnmc,ch->gnhm", onehot, by_distance, preferred_element_type=F32)


def bias_back(lengths, buckets, dtable, rows, heads):
    count = buckets.shape[0]
    labels = (buckets[:, None] == jnp.arange(rows, dtype=jnp.int32)).astype(F32)
    onehot = distance_onehot(lengths, True, count).astype(F32)
    by_distance = jnp.einsum("gnhm,gnmc->ch", dtable, onehot, precision=lax.Precision.HIGHEST)
    grad = jnp.einsum("cb,ch->bh", labels, by_distance, precision=lax.Precision.HIGHEST)
    return grad[:, :heads]


GROUPS = ((0, 1, 2), (3,), (4,))
BACK = ((3,), (2,), (0, 1))
BLOCKS = 4
LINES = 8


def square(dp, fsdp):
    return dp == BLOCKS and fsdp == LINES


def pack(shards):
    qkv, self_out, cross_q, cross_kv, cross_out, ff_in, ff_out, gain_one, gain_two, gain_three, bias = shards
    rows = [gain_one, gain_two, gain_three, bias.reshape(-1)]
    small = jnp.stack([jnp.pad(r, (0, 256 - r.shape[0])) for r in rows])
    small = jnp.pad(small, ((0, 4), (0, 0)))
    return [
        small,
        jnp.concatenate([qkv, cross_q, cross_kv], axis=1),
        jnp.concatenate([self_out, cross_out], axis=0),
        ff_in,
        ff_out,
    ]


def gather_blocks(blocks, dp, fsdp):
    if square(dp, fsdp):
        wholes = gather_all(blocks, GROUPS)
        return [w.reshape((dp, fsdp) + b.shape) for w, b in zip(wholes, blocks)]
    return [lax.all_gather(lax.all_gather(b, "fsdp"), "dp") for b in blocks]


def reduce_blocks(blocks, dp, fsdp):
    if square(dp, fsdp):
        parts = [b.reshape((4, 4, 2) + b.shape[2:]) for b in blocks]
        return reduce_all(parts, BACK)
    return [
        lax.psum_scatter(lax.psum_scatter(b, "dp", scatter_dimension=0), "fsdp", scatter_dimension=0)
        for b in blocks
    ]


def reblock(block, dp, fsdp):
    a, b, rows, columns = block.shape
    matrix = jnp.transpose(block, (1, 2, 0, 3)).reshape(b * rows, a * columns)
    split = matrix.reshape(fsdp, b * rows // fsdp, dp, a * columns // dp)
    return jnp.transpose(split, (2, 0, 1, 3))


def reblock_columns(block, widths, dp, fsdp):
    if block.shape[:2] == (dp, fsdp):
        return block
    total = sum(widths)
    edges, at = [], 0
    for w in widths:
        size = block.shape[3] * w // total
        edges.append((at, at + size))
        at += size
    return jnp.concatenate([reblock(block[..., s:e], dp, fsdp) for s, e in edges], axis=3)


def reblock_rows(block, dp, fsdp):
    if block.shape[:2] == (dp, fsdp):
        return block
    half = block.shape[2] // 2
    return jnp.concatenate([reblock(block[:, :, :half], dp, fsdp), reblock(block[:, :, half:], dp, fsdp)], axis=2)


def reblock_plain(block, dp, fsdp):
    return block if block.shape[:2] == (dp, fsdp) else reblock(block, dp, fsdp)


def joined_rows(block):
    return block.reshape(block.shape[0], block.shape[1] * block.shape[2], block.shape[3])


def split_rows(block, lines):
    return block.reshape(block.shape[0], lines, block.shape[1] // lines, block.shape[2])


def per_device(dec_in, enc_out, d_out, cont_len, buckets, *shards):
    dp, fsdp = lax.axis_size("dp"), lax.axis_size("fsdp")
    small, wide, tall, wi, wo = gather_blocks(pack(shards), dp, fsdp)
    widths = (shards[0].shape[1], shards[2].shape[1], shards[3].shape[1])
    rows = shards[0].shape[0]
    bias_shape = shards[10].shape
    heads = bias_shape[1]
    wide = joined_rows(reblock_columns(wide, widths, BLOCKS, LINES))
    tall = reblock_rows(tall, BLOCKS, LINES)
    wi = joined_rows(reblock_plain(wi, BLOCKS, LINES))
    wo = joined_rows(reblock_plain(wo, BLOCKS, LINES))
    gains = jnp.transpose(small[0, :, :3, :rows], (1, 0, 2)).reshape(3, -1).astype(F32)
    gains = jnp.pad(gains, ((0, 5), (0, 0)))
    bias_rows = small[0, :, 3, : bias_shape[0] * heads].reshape(-1, heads)
    table = bias_tables(cont_len, buckets, bias_rows)
    groups, tokens, width = dec_in.shape
    saved = before(cont_len, dec_in, enc_out, gains, wide, tall, table, heads)
    flat = lambda array: array.reshape(groups * tokens, width)
    out, three, dwi, dwo = feed(flat(saved[-1]), flat(d_out), gains, wi, wo)
    ddec, denc, dgain, dtable, *factors = after(
        cont_len, dec_in, enc_out, gains, wide, tall, table, saved, d_out, three.reshape(dec_in.shape), heads
    )
    dwide, dtall = weights(enc_out, saved[1], saved[5], factors, wide, tall)
    dbias = bias_back(cont_len, buckets, dtable, bias_rows.shape[0], heads)
    vectors = jnp.concatenate([jnp.sum(dgain, axis=0)[:3].reshape(-1), dbias.reshape(-1)])
    vectors = lax.psum(vectors, ("dp", "fsdp"))
    wide, tall, wo, wi = reduce_blocks(
        [
            reblock_columns(split_rows(dwide, LINES), widths, dp, fsdp),
            reblock_rows(dtall, dp, fsdp),
            reblock_plain(split_rows(dwo, LINES), dp, fsdp),
            reblock_plain(split_rows(dwi, LINES), dp, fsdp),
        ],
        dp,
        fsdp,
    )
    a, b, e = widths
    half = tall.shape[0] // 2
    me = lax.axis_index("fsdp")
    gain_sums = [lax.dynamic_slice(vectors[k * width : (k + 1) * width], (me * rows,), (rows,)) for k in range(3)]
    bias_sum = lax.dynamic_slice(vectors[3 * width :].reshape(-1, heads), (me * bias_shape[0], 0), bias_shape)
    return (
        out.reshape(dec_in.shape),
        ddec,
        denc,
        wide[:, :a].astype(F32),
        tall[:half].astype(F32),
        wide[:, a : a + b].astype(F32),
        wide[:, a + b :].astype(F32),
        tall[half:].astype(F32),
        wi.astype(F32),
        wo.astype(F32),
        *gain_sums,
        bias_sum,
    )


def solution(mesh):
    in_specs = (
        P(("dp", "fsdp"), None, None),
        P(("dp", "fsdp"), None, None),
        P(("dp", "fsdp"), None, None),
        P(("dp", "fsdp"), None),
        P(),
        P("fsdp", "dp"),
        P("fsdp", "dp"),
        P("fsdp", "dp"),
        P("fsdp", "dp"),
        P("fsdp", "dp"),
        P("fsdp", "dp"),
        P("fsdp", "dp"),
        P("fsdp"),
        P("fsdp"),
        P("fsdp"),
        P("fsdp", None),
    )
    out_specs = (
        P(("dp", "fsdp"), None, None),
        P(("dp", "fsdp"), None, None),
        P(("dp", "fsdp"), None, None),
        P("fsdp", "dp"),
        P("fsdp", "dp"),
        P("fsdp", "dp"),
        P("fsdp", "dp"),
        P("fsdp", "dp"),
        P("fsdp", "dp"),
        P("fsdp", "dp"),
        P("fsdp"),
        P("fsdp"),
        P("fsdp"),
        P("fsdp", None),
    )
    return jax.shard_map(
        per_device, mesh=mesh, in_specs=in_specs, out_specs=out_specs, check_vma=False
    )
```
